32 devices in a mesh: rows: 8 (over z, y), hid: 4 (over x, core).
Axes of the slice: x: 2, y: 2, z: 4, core: 2. Of those that a mesh axis runs over, the one named last changes fastest.
Arguments:
- ratings: bfloat16 [320, 128, 128], P('rows'), may hold values from -4 to 4, as said below
- tile_user: int32 [320], P('rows'), may hold values from 0 to 7
- tile_item: int32 [320], P('rows'), may hold values from 0 to 31
- tile_seed: int32 [320], P('rows'), may hold values from 0 to 65535
- tile_count: int32 [8], P('rows'), may hold values from 10 to 40, as said below
- item_weight: bfloat16 [32768, 1024], P('rows', 'hid'), may hold values from -0.5 to 0.5
- up_weight: bfloat16 [1024, 4096], P(None, 'hid'), may hold values from -0.1875 to 0.1875
- down_weight: bfloat16 [4096, 1024], P('hid'), may hold values from -0.09375 to 0.09375
Outputs:
- item_grad: bfloat16 [32768, 1024], P('rows', 'hid')
The draws below stay inside these ranges and needn't reach their ends.
Inputs may be any that keep to these rules, and one draw needn't show every extreme that they name: `ratings`: unobserved entries are exactly zero; about half of the entries are observed. Tiles of index r of rows at positions tile_count[r] and beyond are padding; some index has all 40 tiles live in every draw.
All inputs are finite; a program needn't handle non-finite values.
Results may differ from the reference program's by a relative error of at most 0.019.
Values may be sent and summed in bfloat16 or wider, within the bound.
No kernel may reach another device: no remote copies, remote signals or barrier semaphores. Data moves between devices by JAX's collectives and lax.ppermute only.
A program may use at most 64 MiB of HBM per device.

```python
import jax
import jax.numpy as jnp
from jax import lax

D = 1024
FF = 4096
BLK = 128
ITEM_ROW = 4096
TILE_CAP = 40
IBLK_ROW = 32
TILES = 320
USERS = 1024
ITEMS = 32768
N_ROWS = 8


def draw_ratings(key, part):
    first_key, second_key = jax.random.split(key)
    observed = jax.random.randint(first_key, (TILES, BLK, BLK), 0, 2)
    values = jnp.clip(jax.random.normal(second_key, (TILES, BLK, BLK), jnp.float32), -4.0, 4.0)
    return jnp.where(observed == 1, values, jnp.zeros_like(values)).astype(jnp.bfloat16)


def draw_tile_count(key, part):
    first_key, second_key = jax.random.split(key)
    halvings = jax.random.randint(first_key, (N_ROWS,), 0, 3).astype(jnp.int32)
    counts = jnp.right_shift(jnp.full((N_ROWS,), TILE_CAP, jnp.int32), halvings)
    busiest = jax.random.randint(second_key, (), 0, N_ROWS)
    return jnp.where(jnp.arange(N_ROWS) == busiest, TILE_CAP, counts).astype(jnp.int32)


def place_ends(result, own_key, smallest, top_value):
    longest = result.shape.index(max(result.shape))
    spots = []
    for shift in (0, 1):
        where = [jax.random.randint(jax.random.fold_in(own_key, axis), (), 0, length) for axis, length in enumerate(result.shape)]
        where[longest] = (where[longest] + shift) % result.shape[longest]
        spots.append(tuple(where))
    return result.at[spots[0]].set(smallest).at[spots[1]].set(top_value)


def block_levels(own_key, dims, pieces, low, high):
    def one(axis_at, blocks):
        heights = jax.random.uniform(jax.random.fold_in(jax.random.fold_in(own_key, 6), axis_at), (blocks,), jnp.float32, low / len(pieces), high / len(pieces))
        return jnp.repeat(jnp.exp(heights), dims[axis_at] // blocks).reshape((-1,) + (1,) * (len(dims) - axis_at - 1))

    factor_of = one(*pieces[0])
    for cut in pieces[1:]:
        factor_of = factor_of * one(*cut)
    return factor_of


def centred(own_key, shape, scale, bound, cuts=(), held_as=jnp.bfloat16):
    array = scale * jax.random.normal(own_key, shape, jnp.float32)
    if cuts:
        array = array * block_levels(own_key, shape, cuts, -0.22, 0.18)
    return jnp.clip(array, -bound, bound).astype(held_as)


def setup_inputs(seed: int = 0) -> dict:
    key_of = jax.random.split(jax.random.key(seed), 9)
    ratings = draw_ratings(jax.random.fold_in(key_of[8], 71), 0)
    tile_user = place_ends(jax.random.randint(key_of[1], (TILES,), 0, N_ROWS), jax.random.fold_in(key_of[1], 1), 0, N_ROWS - 1).astype(jnp.int32)
    tile_item = place_ends(jax.random.randint(key_of[2], (TILES,), 0, IBLK_ROW), jax.random.fold_in(key_of[2], 1), 0, IBLK_ROW - 1).astype(jnp.int32)
    tile_seed = place_ends(jax.random.randint(key_of[3], (TILES,), 0, 65536), jax.random.fold_in(key_of[3], 1), 0, 65535).astype(jnp.int32)
    tile_count = draw_tile_count(jax.random.fold_in(key_of[8], 71), 0)
    item_weight = centred(key_of[5], (ITEMS, D), BLK ** -0.5, 0.5, ((0, 8), (1, 4)))
    up_weight = centred(key_of[6], (D, FF), D ** -0.5, 0.1875, ((1, 4),))
    down_weight = centred(key_of[7], (FF, D), FF ** -0.5, 0.09375, ((0, 4),))
    return dict(ratings=ratings, tile_user=tile_user, tile_item=tile_item, tile_seed=tile_seed, tile_count=tile_count, item_weight=item_weight, up_weight=up_weight, down_weight=down_weight)


def keep_tiles(seeds):
    offsets = jnp.arange(BLK, dtype=jnp.int32)
    hashed = seeds[:, None, None] * (BLK * BLK) + offsets[None, :, None] * BLK + offsets[None, None, :]
    hashed = hashed * 1597334677
    hashed = hashed ^ lax.shift_right_logical(hashed, jnp.int32(15))
    hashed = hashed * 668265263
    hashed = hashed ^ lax.shift_right_logical(hashed, jnp.int32(13))
    return lax.shift_right_logical(hashed, jnp.int32(7)) & 3 != 0

def prepare(row_ratings, row_items, row_seeds, row_count, row_blocks):
    position = jnp.arange(TILE_CAP, dtype=jnp.int32)
    is_live = position < row_count
    kept = keep_tiles(row_seeds) & is_live[:, None, None]
    corrupted = jnp.where(kept, row_ratings, jnp.zeros_like(row_ratings))
    weights = row_blocks[row_items]
    return (is_live, corrupted, weights)

def errors(row_ratings, is_live, weights, tile_codes):
    predicted = jnp.einsum('tud,tid->tui', tile_codes.astype(jnp.float32), weights.astype(jnp.float32))
    observed = is_live[:, None, None] & (row_ratings != 0)
    scaled = 0.125 * (predicted - row_ratings.astype(jnp.float32))
    return jnp.where(observed, scaled, jnp.zeros_like(scaled)).astype(jnp.bfloat16)

def reference(ratings, tile_user, tile_item, tile_seed, tile_count, item_weight, up_weight, down_weight):
    blocks = item_weight.reshape(N_ROWS, IBLK_ROW, BLK, D)
    rating_rows = ratings.reshape(N_ROWS, TILE_CAP, BLK, BLK)
    user_rows = tile_user.reshape(N_ROWS, TILE_CAP)
    item_rows = tile_item.reshape(N_ROWS, TILE_CAP)
    seed_rows = tile_seed.reshape(N_ROWS, TILE_CAP)
    inputs = (rating_rows, user_rows, item_rows, seed_rows, tile_count, blocks)

    def encode(carry, row_inputs):
        row_ratings, row_users, row_items, row_seeds, row_count, row_blocks = row_inputs
        is_live, corrupted, weights = prepare(row_ratings, row_items, row_seeds, row_count, row_blocks)
        encoded = jnp.einsum('tui,tid->tud', corrupted.astype(jnp.float32), weights.astype(jnp.float32))
        return (carry + jax.ops.segment_sum(encoded, row_users, num_segments=N_ROWS), None)
    code_blocks, _ = lax.scan(encode, jnp.zeros((N_ROWS, BLK, D), jnp.float32), inputs)
    code = code_blocks.reshape(USERS, D)
    root = jnp.sqrt(lax.optimization_barrier(jnp.mean(code * code, axis=1, keepdims=True)) + 1e-05)
    normed = code / root
    normed_b = normed.astype(jnp.bfloat16)
    gate_input = jnp.dot(normed_b, up_weight, preferred_element_type=jnp.float32)
    hidden = jax.nn.silu(gate_input).astype(jnp.bfloat16)
    decoded = jnp.dot(hidden, down_weight, preferred_element_type=jnp.float32).astype(jnp.bfloat16)
    decoded_blocks = decoded.reshape(N_ROWS, BLK, D)

    def back_codes(carry, row_inputs):
        row_ratings, row_users, row_items, row_seeds, row_count, row_blocks = row_inputs
        is_live, corrupted, weights = prepare(row_ratings, row_items, row_seeds, row_count, row_blocks)
        dpred = errors(row_ratings, is_live, weights, decoded_blocks[row_users])
        backward = jnp.einsum('tui,tid->tud', dpred.astype(jnp.float32), weights.astype(jnp.float32))
        return (carry + jax.ops.segment_sum(backward, row_users, num_segments=N_ROWS), None)
    grad_blocks, _ = lax.scan(back_codes, jnp.zeros((N_ROWS, BLK, D), jnp.float32), inputs)
    grad_codes = grad_blocks.reshape(USERS, D).astype(jnp.bfloat16)
    logistic = jax.nn.sigmoid(gate_input)
    hidden_grad = jnp.dot(grad_codes, down_weight.T, preferred_element_type=jnp.float32)
    dgate = (hidden_grad * logistic * (1.0 + gate_input * (1.0 - logistic))).astype(jnp.bfloat16)
    dnorm = jnp.dot(dgate, up_weight.T, preferred_element_type=jnp.float32)
    along = lax.optimization_barrier(jnp.mean(dnorm * normed, axis=1, keepdims=True))
    dcode = ((dnorm - normed * along) / root).astype(jnp.bfloat16)
    dcode_blocks = dcode.reshape(N_ROWS, BLK, D)

    def item_grads(carry, row_inputs):
        row_ratings, row_users, row_items, row_seeds, row_count, row_blocks = row_inputs
        is_live, corrupted, weights = prepare(row_ratings, row_items, row_seeds, row_count, row_blocks)
        tile_codes = decoded_blocks[row_users]
        dpred = errors(row_ratings, is_live, weights, tile_codes)
        per_tile = jnp.einsum('tui,tud->tid', dpred.astype(jnp.float32), tile_codes.astype(jnp.float32))
        per_tile = per_tile + jnp.einsum('tui,tud->tid', corrupted.astype(jnp.float32), dcode_blocks[row_users].astype(jnp.float32))
        row_grad = jax.ops.segment_sum(per_tile, row_items, num_segments=IBLK_ROW)
        return (carry, row_grad.reshape(ITEM_ROW, D).astype(jnp.bfloat16))
    _, grads = lax.scan(item_grads, jnp.zeros((), jnp.float32), inputs)
    return grads.reshape(ITEMS, D)
```

```python
import functools

import jax
import jax.numpy as jnp
from jax import lax
from jax.experimental import pallas as pl
from jax.experimental.pallas import tpu as pltpu
from jax.sharding import PartitionSpec as P

BLK = 128
F32 = jnp.float32
BF16 = jnp.bfloat16


VM = pl.BlockSpec(memory_space=pltpu.VMEM)
SM = pl.BlockSpec(memory_space=pltpu.SMEM)
NT = (((1,), (1,)), ((), ()))
TN = (((0,), (0,)), ((), ()))


def call(body, outs, ins, name, scratch=()):
    specs = [SM if x.dtype == jnp.int32 else VM for x in ins]
    return pl.pallas_call(
        body,
        out_shape=outs,
        in_specs=specs,
        out_specs=jax.tree.map(lambda _: VM, outs),
        scratch_shapes=list(scratch),
        name=name,
    )(*ins)


def sds(shape, dtype):
    return jax.ShapeDtypeStruct(shape, dtype)


def dot(a, b, dims=(((1,), (0,)), ((), ()))):
    return lax.dot_general(a, b, dims, preferred_element_type=F32)


def block(index):
    return pl.ds(pl.multiple_of(index * BLK, BLK), BLK)


def unrolled(total):
    for step in (5, 4, 2):
        if total % step == 0:
            return step
    return 1


def encode(total, rows, meta, ratings, weight, *refs):
    own, rest, corrupted, acc = refs[0], refs[1:rows], refs[rows], refs[rows + 1]
    acc[...] = jnp.zeros_like(acc)
    row = lax.broadcasted_iota(jnp.int32, (BLK, BLK), 0)
    col = lax.broadcasted_iota(jnp.int32, (BLK, BLK), 1)
    base = (row * BLK + col) * jnp.int32(1597334677)
    count = meta[3 * total]

    def step(tile, carry):
        hashed = base + meta[2 * total + tile]
        hashed = hashed ^ lax.shift_right_logical(hashed, jnp.int32(15))
        hashed = hashed * jnp.int32(668265263)
        hashed = hashed ^ lax.shift_right_logical(hashed, jnp.int32(13))
        bits = jnp.where(tile < count, jnp.int32(3 << 7), jnp.int32(0))
        kept = (hashed & bits) != 0
        values = jnp.where(kept, ratings[tile].astype(F32), 0.0).astype(BF16)
        corrupted[tile] = values
        acc[meta[tile]] += dot(values, weight[block(meta[total + tile]), :])
        return carry

    lax.fori_loop(0, total, step, 0, unroll=unrolled(total))
    own[...] = acc[0]
    for k in range(1, rows):
        rest[k - 1][...] = acc[k].astype(BF16)


def network(hids, meta, *refs):
    pieces, up, down = refs[:hids], refs[hids], refs[hids + 1]
    own, rest = refs[hids + 2], refs[hids + 3 : 2 * hids + 2]
    gate_ref, normed_ref, root_ref, wide = refs[2 * hids + 2 :]
    me = meta[meta.shape[0] - 1]
    columns = pieces[0].shape[1]
    features = columns * hids
    codes = [p[...].astype(F32) for p in pieces]
    square = sum(jnp.sum(c * c, axis=1, keepdims=True) for c in codes)
    root = jnp.sqrt(square / features + 1e-05)
    gate = None
    for k in range(hids):
        normed = codes[k] / root
        if k == 0:
            normed_ref[...] = normed
        at = pl.ds(pl.multiple_of((me ^ k) * columns, BLK), columns)
        part = dot(normed.astype(BF16), up[at, :])
        gate = part if gate is None else gate + part
    root_ref[...] = jnp.broadcast_to(root, root_ref.shape)
    gate_ref[...] = gate
    hidden = (gate / (1.0 + jnp.exp(-gate))).astype(BF16)
    decoded = dot(hidden, down[...])
    for k in range(hids):
        wide[k] = decoded[:, k * columns : (k + 1) * columns]
    own[...] = wide[me]
    for k in range(1, hids):
        rest[k - 1][...] = wide[me ^ k].astype(BF16)


def predict(total, rows, hids, meta, weight, *refs):
    blocks, outs, codes = refs[:rows], refs[rows : rows + hids], refs[rows + hids]
    me = meta[meta.shape[0] - 1]
    per = total // hids
    for k in range(rows):
        codes[k] = blocks[k][...]
    for k in range(hids - 1, -1, -1):
        first = (me ^ k) * per

        def step(j, carry, k=k, first=first):
            tile = first + j
            outs[k][j] = dot(
                codes[meta[tile]], weight[block(meta[total + tile]), :], NT
            ).astype(outs[k].dtype)
            return carry

        lax.fori_loop(0, per, step, 0, unroll=unrolled(per))


def backward(total, rows, hids, meta, weight, *refs):
    dpreds, own, rest, acc = refs[:hids], refs[hids], refs[hids + 1 : hids + rows], refs[hids + rows]
    me = meta[meta.shape[0] - 1]
    per = total // hids
    acc[...] = jnp.zeros_like(acc)
    for k in range(hids):
        first = (me ^ k) * per

        def step(j, carry, k=k, first=first):
            tile = first + j
            acc[meta[tile]] += dot(dpreds[k][j], weight[block(meta[total + tile]), :])
            return carry

        lax.fori_loop(0, per, step, 0, unroll=unrolled(per))
    own[...] = acc[0]
    for k in range(1, rows):
        rest[k - 1][...] = acc[k].astype(BF16)


def network_back(hids, meta, *refs):
    grads, pieces = refs[:hids], refs[hids : 2 * hids]
    gate_ref, root_ref, up, down = refs[2 * hids : 2 * hids + 4]
    outs, wide, own_inner = refs[2 * hids + 4 : 3 * hids + 4], refs[3 * hids + 4], refs[3 * hids + 5]
    me = meta[meta.shape[0] - 1]
    columns = pieces[0].shape[1]
    back = None
    for k in range(hids):
        at = pl.ds(pl.multiple_of((me ^ k) * columns, BLK), columns)
        part = dot(grads[k][...], down[:, at], NT)
        back = part if back is None else back + part
    gate = gate_ref[...]
    logistic = 1.0 / (1.0 + jnp.exp(-gate))
    dgate = (back * logistic * (1.0 + gate * (1.0 - logistic))).astype(BF16)
    dnorm = dot(dgate, up[...], NT)
    for k in range(hids):
        wide[k] = dnorm[:, k * columns : (k + 1) * columns]
    root = root_ref[:, :1]
    inner = None
    for k in range(hids):
        piece = wide[me ^ k]
        part = jnp.sum(piece * (pieces[k][...].astype(F32) / root), axis=1, keepdims=True)
        inner = part if inner is None else inner + part
        outs[k][:BLK, :] = piece.astype(outs[k].dtype)
    across = jnp.broadcast_to(inner, (BLK, BLK)).T
    high = across[:8].astype(BF16).astype(F32)
    low = across[:8] - high
    rows = jnp.concatenate([high, low], axis=0)
    for k in range(hids):
        for c in range(columns // BLK):
            outs[k][BLK:, c * BLK : (c + 1) * BLK] = rows.astype(outs[k].dtype)


def finish(hids, features, *refs):
    parts, normed_ref, root_ref, out = refs[:hids], refs[hids], refs[hids + 1], refs[hids + 2]
    total = parts[0][...].astype(F32)
    for p in parts[1:]:
        total = total + p[...].astype(F32)
    split = total[BLK:, :BLK]
    line = split[:1] + split[8:9]
    inner = jnp.broadcast_to(line, (BLK, BLK)).T[:, :1]
    root = root_ref[:, :1]
    out[...] = ((total[:BLK] - normed_ref[...] * (inner / features)) / root).astype(BF16)


def items(total, rows, hids, meta, corrupted, *refs):
    dpreds, codes, grads = refs[:hids], refs[hids : hids + rows], refs[hids + rows : hids + 2 * rows]
    out, acc, both = refs[hids + 2 * rows :]
    me = meta[meta.shape[0] - 1]
    per = total // hids
    acc[...] = jnp.zeros_like(acc)
    for k in range(rows):
        both[k, :BLK, :] = codes[k][...]
        both[k, BLK:, :] = grads[k][...]
    for k in range(hids):
        first = (me ^ k) * per

        def step(j, carry, k=k, first=first):
            tile = first + j
            left = jnp.concatenate([dpreds[k][j], corrupted[tile]], axis=0)
            acc[block(meta[total + tile]), :] += dot(left, both[meta[tile]], TN)
            return carry

        lax.fori_loop(0, per, step, 0, unroll=unrolled(per))
    out[...] = acc[...].astype(out.dtype)


def summed(parts):
    total = parts[0].astype(F32)
    for p in parts[1:]:
        total = total + p.astype(F32)
    return total


def local(
    ratings, tile_user, tile_item, tile_seed, tile_count, item_weight, up_weight, down_weight
):
    total = ratings.shape[0]
    columns = item_weight.shape[1]
    rows = lax.axis_size("rows")
    hids = lax.axis_size("hid")
    features = columns * hids
    hidden = up_weight.shape[1]
    per = total // hids
    row = lax.axis_index("rows")
    hid = lax.axis_index("hid")

    def across(axis, size, value, k):
        return lax.ppermute(value, axis, [(i, i ^ k) for i in range(size)])

    over_rows = functools.partial(across, "rows", rows)
    over_hid = functools.partial(across, "hid", hids)

    def gather(over, size, value):
        return [value] + [over(value, k) for k in range(1, size)]

    def exchange(over, values):
        return [values[0]] + [over(v, k) for k, v in enumerate(values) if k]

    meta = jnp.concatenate(
        [
            tile_user ^ row,
            tile_item,
            tile_seed * jnp.int32(BLK * BLK) * jnp.int32(1597334677),
            tile_count,
            hid[None].astype(jnp.int32),
        ]
    )
    slab = (BLK, columns)
    row_blocks = [sds(slab, F32)] + [sds(slab, BF16)] * (rows - 1)
    row_acc = pltpu.VMEM((rows,) + slab, F32)

    encoded = call(
        functools.partial(encode, total, rows),
        row_blocks + [sds(ratings.shape, BF16)],
        [meta, ratings, item_weight],
        "encode",
        [row_acc],
    )
    corrupted = encoded[rows]
    code = summed(exchange(over_rows, encoded[:rows])).astype(BF16)
    codes = gather(over_hid, hids, code)
    net = call(
        functools.partial(network, hids),
        [sds(slab, F32)]
        + [sds(slab, BF16)] * (hids - 1)
        + [sds((BLK, hidden), F32), sds(slab, F32), sds(slab, F32)],
        [meta, *codes, up_weight, down_weight],
        "network",
        [pltpu.VMEM((hids,) + slab, F32)],
    )
    gate, normed, root = net[hids:]
    decoded = summed(exchange(over_hid, net[:hids])).astype(BF16)
    decoded_all = gather(over_rows, rows, decoded)
    group = (per, BLK, BLK)
    preds = call(
        functools.partial(predict, total, rows, hids),
        [sds(group, F32)] + [sds(group, BF16)] * (hids - 1),
        [meta, item_weight, *decoded_all],
        "predict",
        [pltpu.VMEM((rows,) + slab, BF16)],
    )
    chip = [summed([preds[k], over_hid(preds[k + 1], 1)]) for k in range(0, hids, 2)]
    pred = summed([chip[0]] + [over_hid(chip[j].astype(BF16), 2 * j) for j in range(1, hids // 2)])
    own_ratings = lax.dynamic_slice_in_dim(ratings, hid * per, per, 0)
    position = hid * per + jnp.arange(per, dtype=jnp.int32)
    seen = (own_ratings != 0) & (position < tile_count[0])[:, None, None]
    scaled = 0.125 * (pred - own_ratings.astype(F32))
    dpred = jnp.where(seen, scaled, 0.0).astype(BF16)
    near = [dpred] + [over_hid(dpred, 2 * j) for j in range(1, hids // 2)]
    dpreds = []
    for value in near:
        dpreds += [value, over_hid(value, 1)]
    back = call(
        functools.partial(backward, total, rows, hids),
        row_blocks,
        [meta, item_weight, *dpreds],
        "backward",
        [row_acc],
    )
    code_grad = summed(exchange(over_rows, back)).astype(BF16)
    code_grads = gather(over_hid, hids, code_grad)
    tall = (BLK + 16, columns)
    parts = call(
        functools.partial(network_back, hids),
        [sds(tall, F32)] + [sds(tall, BF16)] * (hids - 1),
        [meta, *code_grads, *codes, gate, root, up_weight, down_weight],
        "network_back",
        [pltpu.VMEM((hids,) + slab, F32), pltpu.VMEM((8, BLK), F32)],
    )
    dcode = call(
        functools.partial(finish, hids, features),
        sds(slab, BF16),
        [*exchange(over_hid, parts), normed, root],
        "finish",
    )
    dcodes = gather(over_rows, rows, dcode)
    return call(
        functools.partial(items, total, rows, hids),
        sds(item_weight.shape, BF16),
        [meta, corrupted, *dpreds, *decoded_all, *dcodes],
        "items",
        [
            pltpu.VMEM(item_weight.shape, F32),
            pltpu.VMEM((rows, 2 * BLK, columns), BF16),
        ],
    )


def solution(mesh):
    placed = (
        P("rows", None, None),
        P("rows"),
        P("rows"),
        P("rows"),
        P("rows"),
        P("rows", "hid"),
        P(None, "hid"),
        P("hid", None),
    )
    return jax.shard_map(
        local, mesh=mesh, in_specs=placed, out_specs=P("rows", "hid"), check_vma=False
    )
```

```python
import functools

import jax
import jax.numpy as jnp
from jax import lax
from jax.experimental import pallas as pl
from jax.experimental.pallas import tpu as pltpu
from jax.sharding import PartitionSpec as P

BLK = 128
F32 = jnp.float32
BF16 = jnp.bfloat16


VM = pl.BlockSpec(memory_space=pltpu.VMEM)
SM = pl.BlockSpec(memory_space=pltpu.SMEM)
NT = (((1,), (1,)), ((), ()))
TN = (((0,), (0,)), ((), ()))


def call(body, outs, ins, name, scratch=()):
    specs = [SM if x.dtype == jnp.int32 else VM for x in ins]
    return pl.pallas_call(
        body,
        out_shape=outs,
        in_specs=specs,
        out_specs=jax.tree.map(lambda _: VM, outs),
        scratch_shapes=list(scratch),
        name=name,
        compiler_params=pltpu.CompilerParams(vmem_limit_bytes=24 << 20),
    )(*ins)


def sds(shape, dtype):
    return jax.ShapeDtypeStruct(shape, dtype)


def dot(a, b, dims=(((1,), (0,)), ((), ()))):
    return lax.dot_general(a, b, dims, preferred_element_type=F32)


def block(index):
    return pl.ds(pl.multiple_of(index * BLK, BLK), BLK)


def unrolled(total):
    for step in (5, 4, 2):
        if total % step == 0:
            return step
    return 1


def encode(total, rows, meta, ratings, weight, *refs):
    own, rest, corrupted, acc = refs[0], refs[1:rows], refs[rows], refs[rows + 1]
    acc[...] = jnp.zeros_like(acc)
    row = lax.broadcasted_iota(jnp.int32, (BLK, BLK), 0)
    col = lax.broadcasted_iota(jnp.int32, (BLK, BLK), 1)
    base = (row * BLK + col) * jnp.int32(1597334677)
    count = meta[3 * total]

    def step(tile, carry):
        hashed = base + meta[2 * total + tile]
        hashed = hashed ^ lax.shift_right_logical(hashed, jnp.int32(15))
        hashed = hashed * jnp.int32(668265263)
        hashed = hashed ^ lax.shift_right_logical(hashed, jnp.int32(13))
        bits = jnp.where(tile < count, jnp.int32(3 << 7), jnp.int32(0))
        kept = (hashed & bits) != 0
        values = jnp.where(kept, ratings[tile].astype(F32), 0.0).astype(BF16)
        corrupted[tile] = values
        acc[meta[tile]] += dot(values, weight[block(meta[total + tile]), :])
        return carry

    lax.fori_loop(0, total, step, 0, unroll=unrolled(total))
    own[...] = acc[0]
    for k in range(1, rows):
        rest[k - 1][...] = acc[k].astype(BF16)


def network(hids, meta, *refs):
    pieces, up, down = refs[:hids], refs[hids], refs[hids + 1]
    own, rest = refs[hids + 2], refs[hids + 3 : 2 * hids + 2]
    gate_ref, normed_ref, root_ref, wide = refs[2 * hids + 2 :]
    me = meta[meta.shape[0] - 1]
    columns = pieces[0].shape[1]
    features = columns * hids
    codes = [p[...].astype(F32) for p in pieces]
    square = sum(jnp.sum(c * c, axis=1, keepdims=True) for c in codes)
    root = jnp.sqrt(square / features + 1e-05)
    gate = None
    for k in range(hids):
        normed = codes[k] / root
        if k == 0:
            normed_ref[...] = normed
        at = pl.ds(pl.multiple_of((me ^ k) * columns, BLK), columns)
        part = dot(normed.astype(BF16), up[at, :])
        gate = part if gate is None else gate + part
    root_ref[...] = jnp.broadcast_to(root, root_ref.shape)
    gate_ref[...] = gate
    hidden = (gate / (1.0 + jnp.exp(-gate))).astype(BF16)
    decoded = dot(hidden, down[...])
    for k in range(hids):
        wide[k] = decoded[:, k * columns : (k + 1) * columns]
    own[...] = wide[me]
    for k in range(1, hids):
        rest[k - 1][...] = wide[me ^ k].astype(BF16)


def predict(total, rows, hids, meta, weight, *refs):
    blocks, outs, codes = refs[:rows], refs[rows : rows + hids], refs[rows + hids]
    me = meta[meta.shape[0] - 1]
    per = total // hids
    for k in range(rows):
        codes[k] = blocks[k][...]
    for k in range(hids - 1, -1, -1):
        first = (me ^ k) * per

        def step(j, carry, k=k, first=first):
            tile = first + j
            outs[k][j] = dot(
                codes[meta[tile]], weight[block(meta[total + tile]), :], NT
            ).astype(outs[k].dtype)
            return carry

        lax.fori_loop(0, per, step, 0, unroll=unrolled(per))


def backward(total, rows, hids, meta, weight, *refs):
    dpreds, own, rest, acc = refs[:hids], refs[hids], refs[hids + 1 : hids + rows], refs[hids + rows]
    me = meta[meta.shape[0] - 1]
    per = total // hids
    acc[...] = jnp.zeros_like(acc)
    for k in range(hids):
        first = (me ^ k) * per

        def step(j, carry, k=k, first=first):
            tile = first + j
            acc[meta[tile]] += dot(dpreds[k][j], weight[block(meta[total + tile]), :])
            return carry

        lax.fori_loop(0, per, step, 0, unroll=unrolled(per))
    own[...] = acc[0]
    for k in range(1, rows):
        rest[k - 1][...] = acc[k].astype(BF16)


def network_back(hids, meta, *refs):
    grads, pieces = refs[:hids], refs[hids : 2 * hids]
    gate_ref, root_ref, up, down = refs[2 * hids : 2 * hids + 4]
    outs, wide, own_inner = refs[2 * hids + 4 : 3 * hids + 4], refs[3 * hids + 4], refs[3 * hids + 5]
    me = meta[meta.shape[0] - 1]
    columns = pieces[0].shape[1]
    back = None
    for k in range(hids):
        at = pl.ds(pl.multiple_of((me ^ k) * columns, BLK), columns)
        part = dot(grads[k][...], down[:, at], NT)
        back = part if back is None else back + part
    gate = gate_ref[...]
    logistic = 1.0 / (1.0 + jnp.exp(-gate))
    dgate = (back * logistic * (1.0 + gate * (1.0 - logistic))).astype(BF16)
    dnorm = dot(dgate, up[...], NT)
    for k in range(hids):
        wide[k] = dnorm[:, k * columns : (k + 1) * columns]
    root = root_ref[:, :1]
    inner = None
    for k in range(hids):
        piece = wide[me ^ k]
        part = jnp.sum(piece * (pieces[k][...].astype(F32) / root), axis=1, keepdims=True)
        inner = part if inner is None else inner + part
        outs[k][:BLK, :] = piece.astype(outs[k].dtype)
    across = jnp.broadcast_to(inner, (BLK, BLK)).T
    high = across[:8].astype(BF16).astype(F32)
    low = across[:8] - high
    rows = jnp.concatenate([high, low], axis=0)
    for k in range(hids):
        for c in range(columns // BLK):
            outs[k][BLK:, c * BLK : (c + 1) * BLK] = rows.astype(outs[k].dtype)


def finish(hids, features, *refs):
    parts, normed_ref, root_ref, out = refs[:hids], refs[hids], refs[hids + 1], refs[hids + 2]
    total = parts[0][...].astype(F32)
    for p in parts[1:]:
        total = total + p[...].astype(F32)
    split = total[BLK:, :BLK]
    line = split[:1] + split[8:9]
    inner = jnp.broadcast_to(line, (BLK, BLK)).T[:, :1]
    root = root_ref[:, :1]
    out[...] = ((total[:BLK] - normed_ref[...] * (inner / features)) / root).astype(BF16)


def items(total, rows, hids, meta, corrupted, *refs):
    dpreds, codes, grads = refs[:hids], refs[hids : hids + rows], refs[hids + rows : hids + 2 * rows]
    out, acc, both = refs[hids + 2 * rows :]
    me = meta[meta.shape[0] - 1]
    per = total // hids
    acc[...] = jnp.zeros_like(acc)
    for k in range(rows):
        both[k, :BLK, :] = codes[k][...]
        both[k, BLK:, :] = grads[k][...]
    for k in range(hids):
        first = (me ^ k) * per

        def step(j, carry, k=k, first=first):
            tile = first + j
            left = jnp.concatenate([dpreds[k][j], corrupted[tile]], axis=0)
            acc[block(meta[total + tile]), :] += dot(left, both[meta[tile]], TN)
            return carry

        lax.fori_loop(0, per, step, 0, unroll=unrolled(per))
    out[...] = acc[...].astype(out.dtype)


def summed(parts):
    total = parts[0].astype(F32)
    for p in parts[1:]:
        total = total + p.astype(F32)
    return total


def local(
    ratings, tile_user, tile_item, tile_seed, tile_count, item_weight, up_weight, down_weight
):
    total = ratings.shape[0]
    item_weight = pltpu.with_memory_space_constraint(item_weight, pltpu.VMEM)
    up_weight = pltpu.with_memory_space_constraint(up_weight, pltpu.VMEM)
    down_weight = pltpu.with_memory_space_constraint(down_weight, pltpu.VMEM)
    columns = item_weight.shape[1]
    rows = lax.axis_size("rows")
    hids = lax.axis_size("hid")
    features = columns * hids
    hidden = up_weight.shape[1]
    per = total // hids
    row = lax.axis_index("rows")
    hid = lax.axis_index("hid")

    def across(axis, size, value, k):
        return lax.ppermute(value, axis, [(i, i ^ k) for i in range(size)])

    over_rows = functools.partial(across, "rows", rows)
    over_hid = functools.partial(across, "hid", hids)

    def gather(over, size, value):
        return [value] + [over(value, k) for k in range(1, size)]

    def exchange(over, values):
        return [values[0]] + [over(v, k) for k, v in enumerate(values) if k]

    meta = jnp.concatenate(
        [
            tile_user ^ row,
            tile_item,
            tile_seed * jnp.int32(BLK * BLK) * jnp.int32(1597334677),
            tile_count,
            hid[None].astype(jnp.int32),
        ]
    )
    slab = (BLK, columns)
    row_blocks = [sds(slab, F32)] + [sds(slab, BF16)] * (rows - 1)
    row_acc = pltpu.VMEM((rows,) + slab, F32)

    encoded = call(
        functools.partial(encode, total, rows),
        row_blocks + [sds(ratings.shape, BF16)],
        [meta, ratings, item_weight],
        "encode",
        [row_acc],
    )
    corrupted = encoded[rows]
    code = summed(exchange(over_rows, encoded[:rows])).astype(BF16)
    codes = gather(over_hid, hids, code)
    net = call(
        functools.partial(network, hids),
        [sds(slab, F32)]
        + [sds(slab, BF16)] * (hids - 1)
        + [sds((BLK, hidden), F32), sds(slab, F32), sds(slab, F32)],
        [meta, *codes, up_weight, down_weight],
        "network",
        [pltpu.VMEM((hids,) + slab, F32)],
    )
    gate, normed, root = net[hids:]
    decoded = summed(exchange(over_hid, net[:hids])).astype(BF16)
    decoded_all = gather(over_rows, rows, decoded)
    group = (per, BLK, BLK)
    preds = call(
        functools.partial(predict, total, rows, hids),
        [sds(group, F32)] + [sds(group, BF16)] * (hids - 1),
        [meta, item_weight, *decoded_all],
        "predict",
        [pltpu.VMEM((rows,) + slab, BF16)],
    )
    chip = [summed([preds[k], over_hid(preds[k + 1], 1)]) for k in range(0, hids, 2)]
    pred = summed([chip[0]] + [over_hid(chip[j].astype(BF16), 2 * j) for j in range(1, hids // 2)])
    own_ratings = lax.dynamic_slice_in_dim(ratings, hid * per, per, 0)
    position = hid * per + jnp.arange(per, dtype=jnp.int32)
    seen = (own_ratings != 0) & (position < tile_count[0])[:, None, None]
    scaled = 0.125 * (pred - own_ratings.astype(F32))
    dpred = jnp.where(seen, scaled, 0.0).astype(BF16)
    near = [dpred] + [over_hid(dpred, 2 * j) for j in range(1, hids // 2)]
    dpreds = []
    for value in near:
        dpreds += [value, over_hid(value, 1)]
    back = call(
        functools.partial(backward, total, rows, hids),
        row_blocks,
        [meta, item_weight, *dpreds],
        "backward",
        [row_acc],
    )
    code_grad = summed(exchange(over_rows, back)).astype(BF16)
    code_grads = gather(over_hid, hids, code_grad)
    tall = (BLK + 16, columns)
    parts = call(
        functools.partial(network_back, hids),
        [sds(tall, F32)] + [sds(tall, BF16)] * (hids - 1),
        [meta, *code_grads, *codes, gate, root, up_weight, down_weight],
        "network_back",
        [pltpu.VMEM((hids,) + slab, F32), pltpu.VMEM((8, BLK), F32)],
    )
    dcode = call(
        functools.partial(finish, hids, features),
        sds(slab, BF16),
        [*exchange(over_hid, parts), normed, root],
        "finish",
    )
    dcodes = gather(over_rows, rows, dcode)
    return call(
        functools.partial(items, total, rows, hids),
        sds(item_weight.shape, BF16),
        [meta, corrupted, *dpreds, *decoded_all, *dcodes],
        "items",
        [
            pltpu.VMEM(item_weight.shape, F32),
            pltpu.VMEM((rows, 2 * BLK, columns), BF16),
        ],
    )


def solution(mesh):
    placed = (
        P("rows", None, None),
        P("rows"),
        P("rows"),
        P("rows"),
        P("rows"),
        P("rows", "hid"),
        P(None, "hid"),
        P("hid", None),
    )
    return jax.shard_map(
        local, mesh=mesh, in_specs=placed, out_specs=P("rows", "hid"), check_vma=False
    )
```
